512 devices in a mesh: pole: 8 (over z_lo, core), row: 4 (over x), col: 16 (over y, z_hi).
Axes of the slice: x: 4, y: 8, z: 8 (z_hi: 2, z_lo: 4; z = z_hi * 4 + z_lo), core: 2. Of those that a mesh axis runs over, the one named last changes fastest.
Arguments:
- inverse_block: bfloat16 [8, 2, 16, 4, 64, 4096], P('pole', None, None, 'row', None, 'col'), may hold values from -5 to 5
- panels: bfloat16 [8, 3, 2, 16, 4, 64, 256], P('pole', None, None, 'col', 'row'), may hold values from -0.09375 to 0.09375
- panel_mask: int32 [3, 16, 4], P(None, 'col', 'row'), may hold values 0 or 1
- parent_panels: float32 [8, 2, 2, 256, 256], P('pole'), may hold values from -0.25 to 0.25
- diag_inverse: float32 [8, 3, 2, 256, 256], P('pole'), may hold values from -6 to 6
- pole_weights: float32 [8, 2], P('pole'), may hold values from 0.5 to 1.5
Outputs:
- density_panel: float32 [3, 16, 4, 64, 256], P(None, 'col', 'row', None, 'pole')
- density_diag: float32 [3, 256, 256], replicated
The draws below stay inside these ranges and needn't reach their ends.
Inputs may be any that keep to these rules, and one draw needn't show every extreme that they name: panel_mask[k, a, b] is 1 where the block of 64 ancestor rows (a, b) of supernode k's factor panel may be nonzero, 0 where it is structurally zero.
All inputs are finite; a program needn't handle non-finite values.
Results may differ from the reference program's by a relative error of at most 0.0003.
Values may be sent and summed in bfloat16 or wider, within the bound.
A program may use at most 64 MiB of HBM per device.

```python
import jax
import jax.numpy as jnp
from jax import lax

M = 4096
S = 256
NSUP = 3
POLES = 8
GRID_ROWS = 4
GRID_COLS = 16
BLK = 64


def plant(values, own_key, least, top_value):
    index_at = [jax.random.randint(jax.random.fold_in(own_key, axis), (), 0, length) for axis, length in enumerate(values.shape)]
    main_axis = values.shape.index(max(values.shape))
    neighbour = index_at[:main_axis] + [(index_at[main_axis] + 1) % values.shape[main_axis]] + index_at[main_axis + 1:]
    return values.at[tuple(index_at)].set(least).at[tuple(neighbour)].set(top_value)


def block_levels(rng, extent, split, low, top_value):
    level, own = 1.0, jax.random.fold_in(rng, 6)
    for dim, parts in split:
        steps = jnp.exp(jax.random.uniform(jax.random.fold_in(own, dim), (parts,), jnp.float32, low / len(split), top_value / len(split)))
        level = level * jnp.repeat(steps, extent[dim] // parts).reshape([-1 if axis == dim else 1 for axis in range(len(extent))])
    return level


def normal_values(rng, dims, scale, most, pieces=(), held_as=jnp.bfloat16):
    factor_of = block_levels(rng, dims, pieces, -0.22, 0.18) if pieces else 1.0
    values = jax.random.normal(rng, dims, jnp.float32) * scale * factor_of
    return jnp.minimum(jnp.maximum(values, -most), most).astype(held_as)


def setup_inputs(seed: int = 0) -> dict:
    key_of = jax.random.split(jax.random.key(seed), 7)
    return {
        "inverse_block": normal_values(key_of[0], (POLES, 2, GRID_COLS, GRID_ROWS, BLK, M), 0.8, 5.0, ((0, 8), (3, 4), (5, 16))),
        "panels": normal_values(key_of[1], (POLES, NSUP, 2, GRID_COLS, GRID_ROWS, BLK, S), M ** -0.5, 0.09375, ((0, 8), (3, 16), (4, 4))),
        "panel_mask": plant((jax.random.randint(key_of[2], (NSUP, GRID_COLS, GRID_ROWS), 0, 4) < 3).astype(jnp.int32), jax.random.fold_in(key_of[2], 1), 0, 1),
        "parent_panels": normal_values(key_of[3], (POLES, NSUP - 1, 2, S, S), (2 * S) ** -0.5, 0.25, ((0, 8),), jnp.float32),
        "diag_inverse": normal_values(key_of[4], (POLES, NSUP, 2, S, S), 1.0, 6.0, ((0, 8),), jnp.float32),
        "pole_weights": jnp.clip(0.5 + 1.0 * jax.random.uniform(key_of[5], (POLES, 2), jnp.float32) ** block_levels(key_of[5], (POLES, 2), ((0, 8),), -0.2, 0.2), 0.5, 1.5),
    }


def matmul_high(left_side, right_side):
    return jnp.dot(left_side, right_side, precision=lax.Precision.HIGHEST, preferred_element_type=jnp.float32)


def complex_dot(left_real, left_imag, right_real, right_imag):
    real_part = matmul_high(left_real, right_real) - matmul_high(left_imag, right_imag)
    imag_part = matmul_high(left_real, right_imag) + matmul_high(left_imag, right_real)
    return real_part, imag_part


def panel_columns(flat_panels):
    stack_depth = flat_panels.shape[0]
    row_count = flat_panels.shape[2]
    panel_width = flat_panels.shape[3]
    upper_rows = jnp.concatenate([flat_panels[:, 0], flat_panels[:, 1]], axis=-1)
    lower_rows = jnp.concatenate([-flat_panels[:, 1], flat_panels[:, 0]], axis=-1)
    upper_rows = jnp.moveaxis(upper_rows, 0, 1).reshape(row_count, stack_depth * 2 * panel_width)
    lower_rows = jnp.moveaxis(lower_rows, 0, 1).reshape(row_count, stack_depth * 2 * panel_width)
    return upper_rows, lower_rows


def column_product(stored_columns, upper_rows, lower_rows):
    contract_dims = (((0,), (0,)), ((), ()))
    first_term = lax.dot_general(stored_columns[0], upper_rows, contract_dims, preferred_element_type=jnp.float32)
    second_term = lax.dot_general(stored_columns[1], lower_rows, contract_dims, preferred_element_type=jnp.float32)
    return first_term + second_term


def reference(inverse_block, panels, panel_mask, parent_panels, diag_inverse, pole_weights):
    block_flags = jnp.repeat(panel_mask.reshape(NSUP, GRID_COLS * GRID_ROWS), BLK, axis=1).astype(jnp.bfloat16)

    def one_pole(carried, inputs):
        block_part, panel_part, parent, diag_blocks, weight = inputs
        ancestor = block_part.reshape(2, M, M)
        masked = panel_part.reshape(NSUP, 2, M, S) * block_flags[:, None, :, None]
        upper_rows, lower_rows = panel_columns(masked)
        products = column_product(ancestor, upper_rows, lower_rows)
        panel_terms = []
        diag_terms = []
        x_real = None
        x_imag = None
        z_real = None
        z_imag = None
        for level in range(NSUP):
            base_real = products[:, level * 2 * S:level * 2 * S + S]
            base_imag = products[:, level * 2 * S + S:(level + 1) * 2 * S]
            if level == 0:
                x_real = -base_real
                x_imag = -base_imag
            else:
                carry_real, carry_imag = complex_dot(x_real, x_imag, parent[level - 1, 0], parent[level - 1, 1])
                x_real = -(base_real + carry_real)
                x_imag = -(base_imag + carry_imag)
            own_real = masked[level, 0].astype(jnp.float32)
            own_imag = masked[level, 1].astype(jnp.float32)
            sum_real, sum_imag = complex_dot(own_real.T, own_imag.T, x_real, x_imag)
            y_real = diag_blocks[level, 0] - sum_real
            y_imag = diag_blocks[level, 1] - sum_imag
            if level > 0:
                back_real, back_imag = complex_dot(parent[level - 1, 0].T, parent[level - 1, 1].T, z_real, z_imag)
                y_real = y_real - back_real
                y_imag = y_imag - back_imag
            if level + 1 < NSUP:
                next_real = masked[level + 1, 0].astype(jnp.float32)
                next_imag = masked[level + 1, 1].astype(jnp.float32)
                follow_real, follow_imag = complex_dot(next_real.T, next_imag.T, x_real, x_imag)
                mix_real, mix_imag = complex_dot(y_real, y_imag, parent[level, 0], parent[level, 1])
                z_real = -(follow_real.T + mix_real)
                z_imag = -(follow_imag.T + mix_imag)
            panel_terms.append(weight[0] * x_imag + weight[1] * x_real)
            diag_terms.append(weight[0] * y_imag + weight[1] * y_real)
        return (carried[0] + jnp.stack(panel_terms), carried[1] + jnp.stack(diag_terms)), None

    initial = (jnp.zeros((NSUP, M, S), jnp.float32), jnp.zeros((NSUP, S, S), jnp.float32))
    totals, unused = lax.scan(one_pole, initial, (inverse_block, panels, parent_panels, diag_inverse, pole_weights))
    return totals[0].reshape(NSUP, GRID_COLS, GRID_ROWS, BLK, S), totals[1]
```

```python
import jax
import jax.numpy as jnp
from jax import lax
from jax.experimental import pallas as pl
from jax.experimental.pallas import tpu as pltpu
from jax.sharding import Mesh
from jax.sharding import PartitionSpec as P

F32 = jnp.float32
BF16 = jnp.bfloat16
MESH = pl.DeviceIdType.MESH
POLE = ("zl", "core")
COL = ("y", "zh")
NZL, NC, NX, NY, NZH = 4, 2, 4, 8, 2
NZ = NZL * NZH
NQ = NX * NC
NP = NZL * NC
NA = NY * NZH


def split(value):
    high = value.astype(BF16)
    low = (value - high.astype(F32)).astype(BF16)
    return high, low


def dot(left, right):
    return lax.dot_general(left, right, (((1,), (0,)), ((), ())), preferred_element_type=F32)


def dot_exact_left(left, right_high, right_low):
    return dot(left, right_high) + dot(left, right_low)


def dot_split(left, right):
    return dot(left[0], right[0]) + (dot(left[1], right[0]) + dot(left[0], right[1]))


def turned(real, imag):
    upper = jnp.concatenate([real, imag], axis=1)
    lower = jnp.concatenate([imag, -real], axis=1)
    return jnp.concatenate([upper, lower], axis=0)


def kernel(
    inv_ref, pan_ref, mask_ref, par_ref, dia_ref, weight_ref,
    panel_out, diag_out,
    g_in, g_t, par_v, dia_v, gath, near, p_t, q_big, q_t, sent, got,
    pole_sent, pole_got, z_sent, z_got, y_got, z_all, whole,
    load_sem, y_send, y_recv, zh_send, x_send, x_recv, ab_send, ab_recv,
    p_send, p_recv, zr_send, zr_recv, yg_send, yg_recv, zg_send, zg_recv,
    fx_send, fc_send, f_recv,
):
    zl = lax.axis_index("zl")
    core = lax.axis_index("core")
    x = lax.axis_index("x")
    y = lax.axis_index("y")
    zh = lax.axis_index("zh")
    z = zh * NZL + zl
    q = x * NC + core
    pole = zl * NC + core
    own = y * NZH + zh
    other = y * NZH + (1 - zh)

    def remote(source, target, send, recv, **where):
        return pltpu.make_async_remote_copy(
            src_ref=source, dst_ref=target, send_sem=send, recv_sem=recv,
            device_id=where, device_id_type=MESH,
        )

    def each(count, body):
        def step(index, carry):
            body(index)
            return carry
        lax.fori_loop(0, count, step, 0)

    loads = [
        pltpu.make_async_copy(inv_ref, g_in, load_sem.at[0]),
        pltpu.make_async_copy(par_ref, par_v, load_sem.at[1]),
        pltpu.make_async_copy(dia_ref, dia_v, load_sem.at[2]),
    ]
    for load in loads:
        load.start()

    barrier = pltpu.get_barrier_semaphore()

    def greet(**where):
        pl.semaphore_signal(barrier, inc=1, device_id=where, device_id_type=MESH)

    each(NY - 1, lambda i: greet(y=lax.rem(y + 1 + i, NY)))

    def greet_z(i):
        to = lax.rem(z + 1 + i, NZ)
        greet(zl=lax.rem(to, NZL), zh=to // NZL)

    each(NZ - 1, greet_z)

    def greet_q(i):
        to = lax.rem(q + 1 + i, NQ)
        greet(x=to // NC, core=lax.rem(to, NC))

    each(NQ - 1, greet_q)
    each(NZL - 1, lambda i: greet(zl=lax.rem(zl + 1 + i, NZL), core=1 - core))

    for level in range(3):
        flag = mask_ref[level].astype(F32)
        for part in range(2):
            block = (pan_ref[level, part].astype(F32) * flag).astype(BF16)
            gath[level, own, part] = block
            near[level, x, part] = block

    pl.semaphore_wait(barrier, NY - 1 + NZ - 1 + NQ - 1 + NZL - 1)

    def send_zh(level):
        return remote(
            gath.at[level, own], gath.at[level, own], zh_send.at[level], y_recv.at[level, own], zh=1 - zh
        )

    def send_y(level, part, block, i):
        offset = 4 + ((i + 1) // 2) * (1 - 2 * lax.rem(i, 2))
        return remote(
            gath.at[level, block], gath.at[level, block],
            y_send.at[level, part, i], y_recv.at[level, block], y=lax.rem(y + offset, NY),
        )

    def send_x(level, i):
        return remote(
            near.at[level, x], near.at[level, x], x_send.at[level, i], x_recv.at[level, x],
            x=lax.rem(x + 1 + i, NX),
        )

    for level in range(3):
        send_zh(level).start()
    for level in range(3):
        each(NY - 1, lambda i, level=level: send_y(level, 0, own, i).start())
        each(NX - 1, lambda i, level=level: send_x(level, i).start())
        remote(
            gath.at[level, other], gath.at[level, other], zh_send.at[level], y_recv.at[level, other], zh=1 - zh
        ).wait_recv()
        each(NY - 1, lambda i, level=level: send_y(level, 1, other, i).start())

    for load in loads:
        load.wait()
    weight_real = weight_ref[0]
    weight_imag = weight_ref[1]
    for part in range(2):
        g_t[:, part * 1024 : (part + 1) * 1024] = g_in[part].reshape(1024, 256).T
    for step in range(2):
        real = split(par_v[step, 0])
        imag = split(par_v[step, 1])
        for piece in range(2):
            q_big[step, piece, :256, :256] = real[piece]
            q_big[step, piece, :256, 256:] = imag[piece]
            q_big[step, piece, 256:, :256] = -imag[piece]
            q_big[step, piece, 256:, 256:] = real[piece]
            q_t[step, piece, :, :256] = real[piece].T
            q_t[step, piece, :, 256:] = -imag[piece].T
    first = (x == 0) & (y == 0) & (zh == 0)
    leader = jnp.where(first, 1.0, 0.0).astype(F32)

    def wait_x(level, i):
        source = lax.rem(x + 1 + i, NX)
        remote(
            near.at[level, source], near.at[level, source], x_send.at[level, i], x_recv.at[level, source], x=source
        ).wait_recv()

    def wait_y(level, i):
        source = lax.rem(y + 1 + i, NY)
        for half in range(NZH):
            block = source * NZH + half
            remote(
                gath.at[level, block], gath.at[level, block], y_send.at[level, 0, i],
                y_recv.at[level, block], y=source,
            ).wait_recv()

    for level in range(3):
        each(NX - 1, lambda i, level=level: wait_x(level, i))
        p_t[level, :, :256] = near[level, :, 0].reshape(256, 256).T
        p_t[level, :, 256:] = -(near[level, :, 1].reshape(256, 256).T)

    carry = None
    back = None
    for level in range(3):
        each(NY - 1, lambda i, level=level: wait_y(level, i))
        p_real = gath[level, :, 0].reshape(1024, 256)
        p_imag = gath[level, :, 1].reshape(1024, 256)
        g_real = g_t[:, :1024]
        g_imag = g_t[:, 1024:]
        b_real = dot(g_real, p_real) - dot(g_imag, p_imag)
        b_imag = dot(g_real, p_imag) + dot(g_imag, p_real)
        x_real = -(weight_real * b_real - weight_imag * b_imag)
        x_imag = -(weight_real * b_imag + weight_imag * b_real)
        if level > 0:
            x_real = x_real - carry[:, :256]
            x_imag = x_imag - carry[:, 256:]
        d_real = leader * (weight_real * dia_v[level, 0] - weight_imag * dia_v[level, 1])
        d_imag = leader * (weight_real * dia_v[level, 1] + weight_imag * dia_v[level, 0])
        if level < 2:
            x_high, x_low = split(jnp.concatenate([x_real, x_imag], axis=1))
            round_high, round_low = split(turned(x_real, x_imag))
            w_both = dot_exact_left(p_t[level], round_high, round_low)
            y_real = d_real - w_both[:, :256]
            y_imag = d_imag - w_both[:, 256:]
            if level > 0:
                y_real = y_real - back[:, :256]
                y_imag = y_imag - back[:, 256:]
        else:
            columns = jnp.concatenate([x_imag, -x_real], axis=0)
            col_high, col_low = split(columns)
            y_imag = d_imag - dot_exact_left(p_t[level], col_high, col_low) - back[:, 256:]
        for to in range(NQ):
            sent[level, to, :32] = x_imag[32 * to : 32 * to + 32]
            sent[level, to, 32:] = y_imag[32 * to : 32 * to + 32]

        def send_q(i, level=level):
            to = lax.rem(q + 1 + i, NQ)
            remote(
                sent.at[level, to], got.at[level, q], ab_send.at[level, i], ab_recv.at[level, q],
                x=to // NC, core=lax.rem(to, NC),
            ).start()

        each(NQ - 1, send_q)
        if level < 2:
            q_pieces = (q_big[level, 0], q_big[level, 1])
            carry = dot_split((x_high, x_low), q_pieces)
            follow = dot_exact_left(p_t[level + 1], round_high, round_low)
            mix = dot_split(split(jnp.concatenate([y_real, y_imag], axis=1)), q_pieces)
            z_real = -(follow[:, :256].T + mix[:, :256])
            z_imag = -(follow[:, 256:].T + mix[:, 256:])
            back = dot_split((q_t[level, 0], q_t[level, 1]), split(turned(z_real, z_imag)))

    def wait_q(level, i):
        source = lax.rem(q + 1 + i, NQ)
        remote(
            sent.at[level, 0], got.at[level, source], ab_send.at[level, i], ab_recv.at[level, source],
            x=source // NC, core=lax.rem(source, NC),
        ).wait_recv()

    panel_sums = []
    for level in range(3):
        each(NQ - 1, lambda i, level=level: wait_q(level, i))
        got[level, q] = sent[level, q]
        total = got[level, 0]
        for source in range(1, NQ):
            total = total + got[level, source]
        panel_sums.append(total[:32])
        for tile in range(NZ):
            row, column = 8 * (tile // 2), 128 * (tile % 2)
            z_sent[tile, level] = total[32 + row : 40 + row, column : column + 128]

    def send_zr(i):
        to = lax.rem(z + 1 + i, NZ)
        return remote(
            z_sent.at[to], z_got.at[z], zr_send.at[i], zr_recv.at[z], zl=lax.rem(to, NZL), zh=to // NZL
        )

    each(NZ - 1, lambda i: send_zr(i).start())
    panel_sums.append(jnp.zeros((32, 256), F32))
    pole_sent[...] = jnp.concatenate(panel_sums, axis=0).T.reshape(NP, 32, 128)

    def send_p(i):
        to = lax.rem(pole + 1 + i, NP)
        return remote(
            pole_sent.at[to], pole_got.at[pole], p_send.at[i], p_recv.at[pole],
            zl=to // NC, core=lax.rem(to, NC),
        )

    each(NP - 1, lambda i: send_p(i).start())

    def wait_zr(i):
        source = lax.rem(z + 1 + i, NZ)
        remote(
            z_sent.at[0], z_got.at[source], zr_send.at[i], zr_recv.at[source],
            zl=lax.rem(source, NZL), zh=source // NZL,
        ).wait_recv()

    each(NZ - 1, wait_zr)
    z_got[z] = z_sent[z]
    total = z_got[0]
    for source in range(1, NZ):
        total = total + z_got[source]
    y_got[y] = total

    def send_yg(i):
        return remote(
            y_got.at[y], y_got.at[y], yg_send.at[i], yg_recv.at[y], y=lax.rem(y + 1 + i, NY)
        )

    each(NY - 1, lambda i: send_yg(i).start())

    def wait_p(i):
        source = lax.rem(pole + 1 + i, NP)
        remote(
            pole_sent.at[0], pole_got.at[source], p_send.at[i], p_recv.at[source],
            zl=source // NC, core=lax.rem(source, NC),
        ).wait_recv()

    each(NP - 1, wait_p)
    pole_got[pole] = pole_sent[pole]
    for half in range(NC):
        total = pole_got[half]
        for layer in range(1, NZL):
            total = total + pole_got[layer * NC + half]
        rows = total.T
        for level in range(3):
            panel_out[level, 32 * half : 32 * half + 32] = rows[32 * level : 32 * level + 32]

    def wait_yg(i):
        source = lax.rem(y + 1 + i, NY)
        remote(
            y_got.at[source], y_got.at[source], yg_send.at[i], yg_recv.at[source], y=source
        ).wait_recv()

    each(NY - 1, wait_yg)
    total = y_got[0]
    for source in range(1, NY):
        total = total + y_got[source]
    whole[q, z] = total

    def send_zg(i):
        to = lax.rem(z + 1 + i, NZ)
        return remote(
            whole.at[q, z], whole.at[q, z], zg_send.at[i], zg_recv.at[z], zl=lax.rem(to, NZL), zh=to // NZL
        )

    each(NZ - 1, lambda i: send_zg(i).start())

    def wait_zg(i):
        source = lax.rem(z + 1 + i, NZ)
        remote(
            whole.at[q, source], whole.at[q, source], zg_send.at[i], zg_recv.at[source],
            zl=lax.rem(source, NZL), zh=source // NZL,
        ).wait_recv()

    each(NZ - 1, wait_zg)

    def send_fx(i):
        return remote(
            whole.at[q], whole.at[q], fx_send.at[i], f_recv.at[q], x=lax.rem(x + 1 + i, NX)
        )

    def send_fc(i):
        block = lax.rem(x + i, NX) * NC + core
        return remote(
            whole.at[block], whole.at[block], fc_send.at[i], f_recv.at[block], core=1 - core
        )

    def wait_f(block, i):
        remote(
            whole.at[block], whole.at[block], fc_send.at[i], f_recv.at[block], core=1 - core
        ).wait_recv()

    each(NX - 1, lambda i: send_fx(i).start())
    send_fc(0).start()

    def relay(i):
        wait_f(lax.rem(x + 1 + i, NX) * NC + core, 1 + i)
        send_fc(1 + i).start()

    each(NX - 1, relay)
    each(NX, lambda i: wait_f(lax.rem(x + i, NX) * NC + (1 - core), i))
    for source in range(NQ):
        for tile in range(NZ):
            row, column = 32 * source + 8 * (tile // 2), 128 * (tile % 2)
            diag_out[:, row : row + 8, column : column + 128] = whole[source, tile]

    for level in range(3):
        send_zh(level).wait_send()

        def drain(i, level=level):
            send_y(level, 0, own, i).wait_send()
            send_y(level, 1, other, i).wait_send()
            to = lax.rem(q + 1 + i, NQ)
            remote(
                sent.at[level, to], got.at[level, q], ab_send.at[level, i], ab_recv.at[level, q],
                x=to // NC, core=lax.rem(to, NC),
            ).wait_send()

        each(NY - 1, drain)
        each(NX - 1, lambda i, level=level: send_x(level, i).wait_send())

    def drain_tail(i):
        send_zr(i).wait_send()
        send_p(i).wait_send()
        send_yg(i).wait_send()
        send_zg(i).wait_send()

    each(NZ - 1, drain_tail)
    each(NX - 1, lambda i: send_fx(i).wait_send())
    each(NX, lambda i: send_fc(i).wait_send())


def per_device(inverse_block, panels, panel_mask, parent_panels, diag_inverse, pole_weights):
    any_space = pl.BlockSpec(memory_space=pl.ANY)
    vmem = pl.BlockSpec(memory_space=pltpu.VMEM)
    smem = pl.BlockSpec(memory_space=pltpu.SMEM)
    dma = pltpu.SemaphoreType.DMA
    panel, diag = pl.pallas_call(
        kernel,
        out_shape=(
            jax.ShapeDtypeStruct((3, 64, 32), F32),
            jax.ShapeDtypeStruct((3, 256, 256), F32),
        ),
        in_specs=[any_space, vmem, smem, any_space, any_space, smem],
        out_specs=(vmem, vmem),
        scratch_shapes=[
            pltpu.VMEM((2, NA, 64, 256), BF16),
            pltpu.VMEM((256, 2048), BF16),
            pltpu.VMEM((2, 2, 256, 256), F32),
            pltpu.VMEM((3, 2, 256, 256), F32),
            pltpu.VMEM((3, NA, 2, 64, 256), BF16),
            pltpu.VMEM((3, NX, 2, 64, 256), BF16),
            pltpu.VMEM((3, 256, 512), BF16),
            pltpu.VMEM((2, 2, 512, 512), BF16),
            pltpu.VMEM((2, 2, 256, 512), BF16),
            pltpu.VMEM((3, NQ, 64, 256), F32),
            pltpu.VMEM((3, NQ, 64, 256), F32),
            pltpu.VMEM((NP, 32, 128), F32),
            pltpu.VMEM((NP, 32, 128), F32),
            pltpu.VMEM((NZ, 3, 8, 128), F32),
            pltpu.VMEM((NZ, 3, 8, 128), F32),
            pltpu.VMEM((NY, 3, 8, 128), F32),
            pltpu.VMEM((NZ, 3, 8, 128), F32),
            pltpu.VMEM((NQ, NZ, 3, 8, 128), F32),
            dma((3,)), dma((3, 2, NY)), dma((3, NA)), dma((3,)), dma((3, NX)), dma((3, NX)),
            dma((3, NQ)), dma((3, NQ)), dma((NP,)), dma((NP,)), dma((NZ,)), dma((NZ,)),
            dma((NY,)), dma((NY,)), dma((NZ,)), dma((NZ,)), dma((NX,)), dma((NX,)), dma((NQ,)),
        ],
        compiler_params=pltpu.CompilerParams(collective_id=0, has_side_effects=True),
    )(
        inverse_block[0, :, :, 0],
        panels[0, :, :, 0, 0],
        panel_mask[:, 0, 0],
        parent_panels[0],
        diag_inverse[0],
        pole_weights[0],
    )
    return panel[:, None, None], diag


def solution(mesh):
    torus = Mesh(
        mesh.devices.reshape(NZL, NC, NX, NY, NZH), ("zl", "core", "x", "y", "zh")
    )
    placed = (
        P(POLE, None, None, "x", None, COL),
        P(POLE, None, None, COL, "x", None, None),
        P(None, COL, "x"),
        P(POLE, None, None, None, None),
        P(POLE, None, None, None, None),
        P(POLE, None),
    )
    return jax.shard_map(
        per_device,
        mesh=torus,
        in_specs=placed,
        out_specs=(P(None, COL, "x", None, POLE), P()),
        check_vma=False,
    )
```

```python
import jax
import jax.numpy as jnp
from jax import lax
from jax.experimental import pallas as pl
from jax.experimental.pallas import tpu as pltpu
from jax.sharding import Mesh
from jax.sharding import PartitionSpec as P

F32 = jnp.float32
BF16 = jnp.bfloat16
MESH = pl.DeviceIdType.MESH
POLE = ("zl", "core")
COL = ("y", "zh")
NZL, NC, NX, NY, NZH = 4, 2, 4, 8, 2
NZ = NZL * NZH
NQ = NX * NC
NP = NZL * NC
NA = NY * NZH
GROUPS = ((0, 1), (2,))

PLAN = (
    "o20", "p", "o21", "p", "o30", "p", "t10", "p", "o31", "p", "t20", "p", "t11", "p", "o40", "p", "t30",
    "p", "t21", "p", "t40", "p", "o22", "p", "t31", "p", "t12", "p", "o41", "t41", "c", "o32", "c", "t22",
    "c", "o42", "c", "t32", "c", "c", "t42", "c", "c",
)


def split(value):
    high = value.astype(BF16)
    low = (value - high.astype(F32)).astype(BF16)
    return high, low


def dot(left, right):
    return lax.dot_general(left, right, (((1,), (0,)), ((), ())), preferred_element_type=F32)


def dot_exact_left(left, right_high, right_low):
    return dot(left, right_high) + dot(left, right_low)


def dot_split(left, right):
    return dot(left[0], right[0]) + (dot(left[1], right[0]) + dot(left[0], right[1]))


def turned(real, imag):
    upper = jnp.concatenate([real, imag], axis=1)
    lower = jnp.concatenate([imag, -real], axis=1)
    return jnp.concatenate([upper, lower], axis=0)


def kernel(
    inv_ref, pan_ref, mask_ref, par_ref, dia_ref, weight_ref,
    panel_out, diag_out,
    g_in, g_t, par_v, dia_v, gath, near, p_t, q_big, q_t, sent, got,
    pole_sent, pole_got, z_sent_early, z_sent_late, z_got_early, z_got_late,
    y_got_early, y_got_late, whole_early, whole_late,
    load_sem, y_send, y_recv, zh_send, zh_recv, x_send, x_recv, ab_send, ab_recv,
    p_send, p_recv, zr_send, zr_recv, yg_send, yg_recv, zg_send, zg_recv,
    fx_send, fc_send, f_recv,
):
    zl = lax.axis_index("zl")
    core = lax.axis_index("core")
    x = lax.axis_index("x")
    y = lax.axis_index("y")
    zh = lax.axis_index("zh")
    z = zh * NZL + zl
    q = x * NC + core
    pole = zl * NC + core
    own = y * NZH + zh
    other = y * NZH + (1 - zh)

    def remote(source, target, send, recv, **where):
        return pltpu.make_async_remote_copy(
            src_ref=source, dst_ref=target, send_sem=send, recv_sem=recv,
            device_id=where, device_id_type=MESH,
        )

    def each(count, body):
        def step(index, carry):
            body(index)
            return carry
        lax.fori_loop(0, count, step, 0)

    z_sent = (z_sent_early, z_sent_late)
    z_got = (z_got_early, z_got_late)
    y_got = (y_got_early, y_got_late)
    whole = (whole_early, whole_late)

    loads = [
        pltpu.make_async_copy(inv_ref, g_in, load_sem.at[0]),
        pltpu.make_async_copy(par_ref, par_v, load_sem.at[1]),
        pltpu.make_async_copy(dia_ref, dia_v, load_sem.at[2]),
    ]
    for load in loads:
        load.start()

    barrier = pltpu.get_barrier_semaphore()

    def greet(**where):
        pl.semaphore_signal(barrier, inc=1, device_id=where, device_id_type=MESH)

    each(NY - 1, lambda i: greet(y=lax.rem(y + 1 + i, NY)))

    def greet_z(i):
        to = lax.rem(z + 1 + i, NZ)
        greet(zl=lax.rem(to, NZL), zh=to // NZL)

    each(NZ - 1, greet_z)

    def greet_q(i):
        to = lax.rem(q + 1 + i, NQ)
        greet(x=to // NC, core=lax.rem(to, NC))

    each(NQ - 1, greet_q)
    each(NZL - 1, lambda i: greet(zl=lax.rem(zl + 1 + i, NZL), core=1 - core))

    for level in range(3):
        flag = mask_ref[level].astype(F32)
        for part in range(2):
            block = (pan_ref[level, part].astype(F32) * flag).astype(BF16)
            gath[level, own, part] = block
            near[level, x, part] = block

    pl.semaphore_wait(barrier, NY - 1 + NZ - 1 + NQ - 1 + NZL - 1)

    def send_zh(level):
        return remote(
            gath.at[level, own], gath.at[level, own], zh_send.at[level], zh_recv.at[level], zh=1 - zh
        )

    def wait_zh(level):
        remote(
            gath.at[level, other], gath.at[level, other], zh_send.at[level], zh_recv.at[level], zh=1 - zh
        ).wait_recv()

    def hop(level, way, half, distance, behind):
        source = lax.rem(y + (behind if way else NY - behind), NY)
        block = source * NZH + (1 - zh if half else zh)
        place = gath.at[level, block] if distance < 4 else gath.at[level, block, way]
        index = ((level * 2 + way) * 2 + half) * 4 + distance - 1
        return remote(
            place, place, y_send.at[index], y_recv.at[index], y=lax.rem(y + (NY - 1 if way else 1), NY)
        )

    def arrive(level, half, distance):
        for way in range(2):
            hop(level, way, half, distance, distance).wait_recv()

    def push(level, half, distance):
        for way in range(2):
            hop(level, way, half, distance, distance - 1).start()

    def send_x(level, i):
        return remote(
            near.at[level, x], near.at[level, x], x_send.at[level, i], x_recv.at[level, x],
            x=lax.rem(x + 1 + i, NX),
        )

    for level in range(3):
        send_zh(level).start()
        push(level, 0, 1)
    for level in range(3):
        each(NX - 1, lambda i, level=level: send_x(level, i).start())

    def send_q(level, kind, i):
        to = lax.rem(q + 1 + i, NQ)
        return remote(
            sent.at[level, to, kind], got.at[level, q, kind], ab_send.at[level, kind, i], ab_recv.at[level, kind, q],
            x=to // NC, core=lax.rem(to, NC),
        )

    weight_real = weight_ref[0]
    weight_imag = weight_ref[1]
    first = (x == 0) & (y == 0) & (zh == 0)
    leader = jnp.where(first, 1.0, 0.0).astype(F32)

    def wait_x(level, i):
        source = lax.rem(x + 1 + i, NX)
        remote(
            near.at[level, source], near.at[level, source], x_send.at[level, i], x_recv.at[level, source], x=source
        ).wait_recv()

    def prepare():
        for load in loads:
            load.wait()
        for part in range(2):
            for piece in range(4):
                g_t[:, part * 1024 + piece * 256 : part * 1024 + piece * 256 + 256] = (
                    g_in[part, 4 * piece : 4 * piece + 4].reshape(256, 256).T
                )
                if piece % 2:
                    yield
        for step in range(2):
            real = split(par_v[step, 0])
            imag = split(par_v[step, 1])
            for piece in range(2):
                q_big[step, piece, :256, :256] = real[piece]
                q_big[step, piece, :256, 256:] = imag[piece]
                q_big[step, piece, 256:, :256] = -imag[piece]
                q_big[step, piece, 256:, 256:] = real[piece]
                q_t[step, piece, :, :256] = real[piece].T
                q_t[step, piece, :, 256:] = -imag[piece].T
                yield
        for level in range(3):
            each(NX - 1, lambda i, level=level: wait_x(level, i))
            p_t[level, :, :256] = near[level, :, 0].reshape(256, 256).T
            p_t[level, :, 256:] = -(near[level, :, 1].reshape(256, 256).T)
            yield

    def chain():
        carry = None
        back = None
        for level in range(3):
            for half in range(2):
                arrive(level, half, 4)
            p_real = gath[level, :, 0].reshape(1024, 256)
            p_imag = gath[level, :, 1].reshape(1024, 256)
            g_real = g_t[:, :1024]
            g_imag = g_t[:, 1024:]
            b_real = dot(g_real, p_real) - dot(g_imag, p_imag)
            if level < 2:
                yield
            b_imag = dot(g_real, p_imag) + dot(g_imag, p_real)
            x_real = -(weight_real * b_real - weight_imag * b_imag)
            x_imag = -(weight_real * b_imag + weight_imag * b_real)
            if level > 0:
                x_real = x_real - carry[:, :256]
                x_imag = x_imag - carry[:, 256:]
            if level < 2:
                yield
            d_real = leader * (weight_real * dia_v[level, 0] - weight_imag * dia_v[level, 1])
            d_imag = leader * (weight_real * dia_v[level, 1] + weight_imag * dia_v[level, 0])
            if level < 2:
                x_high, x_low = split(jnp.concatenate([x_real, x_imag], axis=1))
                round_high, round_low = split(turned(x_real, x_imag))
                w_both = dot_exact_left(p_t[level], round_high, round_low)
                y_real = d_real - w_both[:, :256]
                y_imag = d_imag - w_both[:, 256:]
                if level > 0:
                    y_real = y_real - back[:, :256]
                    y_imag = y_imag - back[:, 256:]
            else:
                columns = jnp.concatenate([x_imag, -x_real], axis=0)
                col_high, col_low = split(columns)
                y_imag = d_imag - dot_exact_left(p_t[level], col_high, col_low) - back[:, 256:]
            for to in range(NQ):
                sent[level, to, 0] = y_imag[32 * to : 32 * to + 32]
            each(NQ - 1, lambda i, level=level: send_q(level, 0, i).start())
            for to in range(NQ):
                sent[level, to, 1] = x_imag[32 * to : 32 * to + 32]
            each(NQ - 1, lambda i, level=level: send_q(level, 1, i).start())
            if level < 2:
                yield
                q_pieces = (q_big[level, 0], q_big[level, 1])
                carry = dot_split((x_high, x_low), q_pieces)
                yield
                follow = dot_exact_left(p_t[level + 1], round_high, round_low)
                mix = dot_split(split(jnp.concatenate([y_real, y_imag], axis=1)), q_pieces)
                z_real = -(follow[:, :256].T + mix[:, :256])
                z_imag = -(follow[:, 256:].T + mix[:, 256:])
                yield
                back = dot_split((q_t[level, 0], q_t[level, 1]), split(turned(z_real, z_imag)))
                yield

    ready = prepare()
    work = chain()
    for step in PLAN:
        if step == "p":
            next(ready, None)
        elif step == "c":
            next(work, None)
        else:
            half, distance, level = "ot".index(step[0]), int(step[1]), int(step[2])
            if distance == 1:
                wait_zh(level)
            else:
                arrive(level, half, distance - 1)
            push(level, half, distance)
    for _ in ready:
        pass
    for _ in work:
        pass

    def sum_q(level, kind):
        def wait_q(i):
            source = lax.rem(q + 1 + i, NQ)
            remote(
                sent.at[level, 0, kind], got.at[level, source, kind], ab_send.at[level, kind, i],
                ab_recv.at[level, kind, source], x=source // NC, core=lax.rem(source, NC),
            ).wait_recv()

        each(NQ - 1, wait_q)
        got[level, q, kind] = sent[level, q, kind]
        total = got[level, 0, kind]
        for source in range(1, NQ):
            total = total + got[level, source, kind]
        return total

    def send_zr(group, i):
        to = lax.rem(z + 1 + i, NZ)
        return remote(
            z_sent[group].at[to], z_got[group].at[z], zr_send.at[group, i], zr_recv.at[group, z],
            zl=lax.rem(to, NZL), zh=to // NZL,
        )

    def send_yg(group, i):
        return remote(
            y_got[group].at[y], y_got[group].at[y], yg_send.at[group, i], yg_recv.at[group, y],
            y=lax.rem(y + 1 + i, NY),
        )

    def send_zg(group, i):
        to = lax.rem(z + 1 + i, NZ)
        place = whole[group].at[q, z]
        return remote(
            place, place, zg_send.at[group, i], zg_recv.at[group, z], zl=lax.rem(to, NZL), zh=to // NZL
        )

    def send_fx(group, i):
        place = whole[group].at[q]
        return remote(place, place, fx_send.at[group, i], f_recv.at[group, q], x=lax.rem(x + 1 + i, NX))

    def send_fc(group, i):
        block = lax.rem(x + i, NX) * NC + core
        place = whole[group].at[block]
        return remote(place, place, fc_send.at[group, i], f_recv.at[group, block], core=1 - core)

    def wait_f(group, block, i):
        place = whole[group].at[block]
        remote(place, place, fc_send.at[group, i], f_recv.at[group, block], core=1 - core).wait_recv()

    def across_z(group):
        for place, level in enumerate(GROUPS[group]):
            total = sum_q(level, 0)
            for tile in range(NZ):
                row, column = 8 * (tile // 2), 128 * (tile % 2)
                z_sent[group][tile, place] = total[row : row + 8, column : column + 128]
        each(NZ - 1, lambda i: send_zr(group, i).start())

    def across_y(group):
        def wait_zr(i):
            source = lax.rem(z + 1 + i, NZ)
            remote(
                z_sent[group].at[0], z_got[group].at[source], zr_send.at[group, i], zr_recv.at[group, source],
                zl=lax.rem(source, NZL), zh=source // NZL,
            ).wait_recv()

        each(NZ - 1, wait_zr)
        z_got[group][z] = z_sent[group][z]
        total = z_got[group][0]
        for source in range(1, NZ):
            total = total + z_got[group][source]
        y_got[group][y] = total
        each(NY - 1, lambda i: send_yg(group, i).start())

    def back_z(group):
        def wait_yg(i):
            source = lax.rem(y + 1 + i, NY)
            place = y_got[group].at[source]
            remote(place, place, yg_send.at[group, i], yg_recv.at[group, source], y=source).wait_recv()

        each(NY - 1, wait_yg)
        total = y_got[group][0]
        for source in range(1, NY):
            total = total + y_got[group][source]
        whole[group][q, z] = total
        each(NZ - 1, lambda i: send_zg(group, i).start())

    def back_x(group):
        def wait_zg(i):
            source = lax.rem(z + 1 + i, NZ)
            place = whole[group].at[q, source]
            remote(
                place, place, zg_send.at[group, i], zg_recv.at[group, source],
                zl=lax.rem(source, NZL), zh=source // NZL,
            ).wait_recv()

        each(NZ - 1, wait_zg)
        each(NX - 1, lambda i: send_fx(group, i).start())
        send_fc(group, 0).start()

    def back_core(group):
        def relay(i):
            wait_f(group, lax.rem(x + 1 + i, NX) * NC + core, 1 + i)
            send_fc(group, 1 + i).start()

        each(NX - 1, relay)

    def place_diag(group):
        each(NX, lambda i: wait_f(group, lax.rem(x + i, NX) * NC + (1 - core), i))
        for place, level in enumerate(GROUPS[group]):
            for source in range(NQ):
                for tile in range(NZ):
                    row, column = 32 * source + 8 * (tile // 2), 128 * (tile % 2)
                    diag_out[level, row : row + 8, column : column + 128] = whole[group][source, tile, place]

    def send_p(i):
        to = lax.rem(pole + 1 + i, NP)
        return remote(
            pole_sent.at[to], pole_got.at[pole], p_send.at[i], p_recv.at[pole],
            zl=to // NC, core=lax.rem(to, NC),
        )

    def wait_p(i):
        source = lax.rem(pole + 1 + i, NP)
        remote(
            pole_sent.at[0], pole_got.at[source], p_send.at[i], p_recv.at[source],
            zl=source // NC, core=lax.rem(source, NC),
        ).wait_recv()

    def both(stage):
        for group in range(2):
            stage(group)

    both(across_z)
    both(across_y)
    panel_sums = [sum_q(level, 1) for level in range(3)] + [jnp.zeros((32, 256), F32)]
    pole_sent[...] = jnp.concatenate(panel_sums, axis=0).T.reshape(NP, 32, 128)
    each(NP - 1, lambda i: send_p(i).start())
    both(back_z)
    each(NP - 1, wait_p)
    pole_got[pole] = pole_sent[pole]
    for half in range(NC):
        total = pole_got[half]
        for layer in range(1, NZL):
            total = total + pole_got[layer * NC + half]
        for level in range(3):
            panel_out[level, :, 32 * half : 32 * half + 32] = total[:, 32 * level : 32 * level + 32]
    both(back_x)
    both(back_core)
    both(place_diag)

    for level in range(3):
        send_zh(level).wait_send()

        for kind in range(2):
            each(NQ - 1, lambda i, level=level, kind=kind: send_q(level, kind, i).wait_send())
        for half in range(2):
            for distance in range(1, 5):
                for way in range(2):
                    hop(level, way, half, distance, distance - 1).wait_send()
        each(NX - 1, lambda i, level=level: send_x(level, i).wait_send())

    each(NP - 1, lambda i: send_p(i).wait_send())
    for group in range(2):

        def drain(i, group=group):
            send_zr(group, i).wait_send()
            send_yg(group, i).wait_send()
            send_zg(group, i).wait_send()

        each(NZ - 1, drain)
        each(NX - 1, lambda i, group=group: send_fx(group, i).wait_send())
        each(NX, lambda i, group=group: send_fc(group, i).wait_send())


def per_device(inverse_block, panels, panel_mask, parent_panels, diag_inverse, pole_weights):
    any_space = pl.BlockSpec(memory_space=pl.ANY)
    vmem = pl.BlockSpec(memory_space=pltpu.VMEM)
    smem = pl.BlockSpec(memory_space=pltpu.SMEM)
    dma = pltpu.SemaphoreType.DMA
    panel, diag = pl.pallas_call(
        kernel,
        out_shape=(
            jax.ShapeDtypeStruct((3, 32, 64), F32),
            jax.ShapeDtypeStruct((3, 256, 256), F32),
        ),
        in_specs=[any_space, vmem, smem, any_space, any_space, smem],
        out_specs=(vmem, vmem),
        scratch_shapes=[
            pltpu.VMEM((2, NA, 64, 256), BF16),
            pltpu.VMEM((256, 2048), BF16),
            pltpu.VMEM((2, 2, 256, 256), F32),
            pltpu.VMEM((3, 2, 256, 256), F32),
            pltpu.VMEM((3, NA, 2, 64, 256), BF16),
            pltpu.VMEM((3, NX, 2, 64, 256), BF16),
            pltpu.VMEM((3, 256, 512), BF16),
            pltpu.VMEM((2, 2, 512, 512), BF16),
            pltpu.VMEM((2, 2, 256, 512), BF16),
            pltpu.VMEM((3, NQ, 2, 32, 256), F32),
            pltpu.VMEM((3, NQ, 2, 32, 256), F32),
            pltpu.VMEM((NP, 32, 128), F32),
            pltpu.VMEM((NP, 32, 128), F32),
            pltpu.VMEM((NZ, 2, 8, 128), F32),
            pltpu.VMEM((NZ, 1, 8, 128), F32),
            pltpu.VMEM((NZ, 2, 8, 128), F32),
            pltpu.VMEM((NZ, 1, 8, 128), F32),
            pltpu.VMEM((NY, 2, 8, 128), F32),
            pltpu.VMEM((NY, 1, 8, 128), F32),
            pltpu.VMEM((NQ, NZ, 2, 8, 128), F32),
            pltpu.VMEM((NQ, NZ, 1, 8, 128), F32),
            dma((3,)), dma((48,)), dma((48,)), dma((3,)), dma((3,)), dma((3, NX)), dma((3, NX)),
            dma((3, 2, NQ)), dma((3, 2, NQ)), dma((NP,)), dma((NP,)), dma((2, NZ)), dma((2, NZ)),
            dma((2, NY)), dma((2, NY)), dma((2, NZ)), dma((2, NZ)), dma((2, NX)), dma((2, NX)), dma((2, NQ)),
        ],
        compiler_params=pltpu.CompilerParams(collective_id=0, has_side_effects=True),
    )(
        inverse_block[0, :, :, 0],
        panels[0, :, :, 0, 0],
        panel_mask[:, 0, 0],
        parent_panels[0],
        diag_inverse[0],
        pole_weights[0],
    )
    return panel.swapaxes(1, 2)[:, None, None], diag


def solution(mesh):
    torus = Mesh(
        mesh.devices.reshape(NZL, NC, NX, NY, NZH), ("zl", "core", "x", "y", "zh")
    )
    placed = (
        P(POLE, None, None, "x", None, COL),
        P(POLE, None, None, COL, "x", None, None),
        P(None, COL, "x"),
        P(POLE, None, None, None, None),
        P(POLE, None, None, None, None),
        P(POLE, None),
    )
    return jax.shard_map(
        per_device,
        mesh=torus,
        in_specs=placed,
        out_specs=(P(None, COL, "x", None, POLE), P()),
        check_vma=False,
    )
```

```python
import jax
import jax.numpy as jnp
from jax import lax
from jax.experimental import pallas as pl
from jax.experimental.pallas import tpu as pltpu
from jax.sharding import Mesh
from jax.sharding import PartitionSpec as P

F32 = jnp.float32
BF16 = jnp.bfloat16
MESH = pl.DeviceIdType.MESH
POLE = ("zl", "core")
COL = ("y", "zh")
NZL, NC, NX, NY, NZH = 4, 2, 4, 8, 2
NZ = NZL * NZH
NQ = NX * NC
NP = NZL * NC
NA = NY * NZH
GROUPS = ((0, 1), (2,))

PLAN = (
    "o20", "p", "o21", "p", "t10", "p", "o30", "p", "o22", "p", "t20", "p", "t11", "p", "o31", "p", "t30",
    "p", "o40", "p", "t12", "p", "t40", "t21", "o32", "o41", "t22", "c", "t31", "c", "o42", "c", "t32", "c",
    "c", "t41", "c", "t42", "c", "c",
)


def split(value):
    high = value.astype(BF16)
    low = (value - high.astype(F32)).astype(BF16)
    return high, low


def dot(left, right):
    return lax.dot_general(left, right, (((1,), (0,)), ((), ())), preferred_element_type=F32)


def dot_exact_left(left, right_high, right_low):
    return dot(left, right_high) + dot(left, right_low)


def dot_split(left, right):
    return dot(left[0], right[0]) + (dot(left[1], right[0]) + dot(left[0], right[1]))


def turned(real, imag):
    upper = jnp.concatenate([real, imag], axis=1)
    lower = jnp.concatenate([imag, -real], axis=1)
    return jnp.concatenate([upper, lower], axis=0)


def kernel(
    inv_ref, pan_ref, mask_ref, par_ref, dia_ref, weight_ref,
    panel_out, diag_out,
    g_in, g_t, par_v, dia_v, gath, near, p_t, q_big, q_t, sent, got,
    pole_sent, pole_got, z_sent_early, z_sent_late, z_got_early, z_got_late,
    y_got_early, y_got_late, whole_early, whole_late,
    load_sem, y_send, y_recv, zh_send, zh_recv, x_send, x_recv, ab_send, ab_recv,
    p_send, p_recv, zr_send, zr_recv, yg_send, yg_recv, zg_send, zg_recv,
    fx_send, fc_send, f_recv,
):
    zl = lax.axis_index("zl")
    core = lax.axis_index("core")
    x = lax.axis_index("x")
    y = lax.axis_index("y")
    zh = lax.axis_index("zh")
    z = zh * NZL + zl
    q = x * NC + core
    pole = zl * NC + core
    own = y * NZH + zh
    other = y * NZH + (1 - zh)

    def remote(source, target, send, recv, **where):
        return pltpu.make_async_remote_copy(
            src_ref=source, dst_ref=target, send_sem=send, recv_sem=recv,
            device_id=where, device_id_type=MESH,
        )

    def each(count, body):
        def step(index, carry):
            body(index)
            return carry
        lax.fori_loop(0, count, step, 0)

    z_sent = (z_sent_early, z_sent_late)
    z_got = (z_got_early, z_got_late)
    y_got = (y_got_early, y_got_late)
    whole = (whole_early, whole_late)

    loads = [
        pltpu.make_async_copy(inv_ref, g_in, load_sem.at[0]),
        pltpu.make_async_copy(par_ref, par_v, load_sem.at[1]),
        pltpu.make_async_copy(dia_ref, dia_v, load_sem.at[2]),
    ]
    for load in loads:
        load.start()

    barrier = pltpu.get_barrier_semaphore()

    def greet(**where):
        pl.semaphore_signal(barrier, inc=1, device_id=where, device_id_type=MESH)

    each(NY - 1, lambda i: greet(y=lax.rem(y + 1 + i, NY)))

    def greet_z(i):
        to = lax.rem(z + 1 + i, NZ)
        greet(zl=lax.rem(to, NZL), zh=to // NZL)

    each(NZ - 1, greet_z)

    def greet_q(i):
        to = lax.rem(q + 1 + i, NQ)
        greet(x=to // NC, core=lax.rem(to, NC))

    each(NQ - 1, greet_q)
    each(NZL - 1, lambda i: greet(zl=lax.rem(zl + 1 + i, NZL), core=1 - core))

    for level in range(3):
        flag = mask_ref[level].astype(F32)
        for part in range(2):
            block = (pan_ref[level, part].astype(F32) * flag).astype(BF16)
            gath[level, own, part] = block
            near[level, x, part] = block

    pl.semaphore_wait(barrier, NY - 1 + NZ - 1 + NQ - 1 + NZL - 1)

    def send_zh(level):
        return remote(
            gath.at[level, own], gath.at[level, own], zh_send.at[level], zh_recv.at[level], zh=1 - zh
        )

    def wait_zh(level):
        remote(
            gath.at[level, other], gath.at[level, other], zh_send.at[level], zh_recv.at[level], zh=1 - zh
        ).wait_recv()

    def hop(level, way, half, distance, behind):
        source = lax.rem(y + (behind if way else NY - behind), NY)
        block = source * NZH + (1 - zh if half else zh)
        place = gath.at[level, block] if distance < 4 else gath.at[level, block, way]
        index = ((level * 2 + way) * 2 + half) * 4 + distance - 1
        return remote(
            place, place, y_send.at[index], y_recv.at[index], y=lax.rem(y + (NY - 1 if way else 1), NY)
        )

    def arrive(level, half, distance):
        for way in range(2):
            hop(level, way, half, distance, distance).wait_recv()

    def push(level, half, distance):
        for way in range(2):
            hop(level, way, half, distance, distance - 1).start()

    def send_x(level, i):
        return remote(
            near.at[level, x], near.at[level, x], x_send.at[level, i], x_recv.at[level, x],
            x=lax.rem(x + 1 + i, NX),
        )

    for level in range(3):
        send_zh(level).start()
        push(level, 0, 1)
    for level in range(3):
        each(NX - 1, lambda i, level=level: send_x(level, i).start())

    def send_q(level, kind, i):
        to = lax.rem(q + 1 + i, NQ)
        return remote(
            sent.at[level, to, kind], got.at[level, q, kind], ab_send.at[level, kind, i], ab_recv.at[level, kind, q],
            x=to // NC, core=lax.rem(to, NC),
        )

    weight_real = weight_ref[0]
    weight_imag = weight_ref[1]
    first = (x == 0) & (y == 0) & (zh == 0)
    leader = jnp.where(first, 1.0, 0.0).astype(F32)

    def wait_x(level, i):
        source = lax.rem(x + 1 + i, NX)
        remote(
            near.at[level, source], near.at[level, source], x_send.at[level, i], x_recv.at[level, source], x=source
        ).wait_recv()

    def prepare():
        for load in loads:
            load.wait()
        for part in range(2):
            for piece in range(4):
                g_t[:, part * 1024 + piece * 256 : part * 1024 + piece * 256 + 256] = (
                    g_in[part, 4 * piece : 4 * piece + 4].reshape(256, 256).T
                )
                if piece % 2:
                    yield
        for step in range(2):
            real = split(par_v[step, 0])
            imag = split(par_v[step, 1])
            for piece in range(2):
                q_big[step, piece, :256, :256] = real[piece]
                q_big[step, piece, :256, 256:] = imag[piece]
                q_big[step, piece, 256:, :256] = -imag[piece]
                q_big[step, piece, 256:, 256:] = real[piece]
                q_t[step, piece, :, :256] = real[piece].T
                q_t[step, piece, :, 256:] = -imag[piece].T
                yield
        for level in range(3):
            each(NX - 1, lambda i, level=level: wait_x(level, i))
            p_t[level, :, :256] = near[level, :, 0].reshape(256, 256).T
            p_t[level, :, 256:] = -(near[level, :, 1].reshape(256, 256).T)
            yield

    def chain():
        carry = None
        back = None
        for level in range(3):
            for half in range(2):
                arrive(level, half, 4)
            p_real = gath[level, :, 0].reshape(1024, 256)
            p_imag = gath[level, :, 1].reshape(1024, 256)
            g_real = g_t[:, :1024]
            g_imag = g_t[:, 1024:]
            b_real = dot(g_real, p_real) - dot(g_imag, p_imag)
            if level < 2:
                yield
            b_imag = dot(g_real, p_imag) + dot(g_imag, p_real)
            x_real = -(weight_real * b_real - weight_imag * b_imag)
            x_imag = -(weight_real * b_imag + weight_imag * b_real)
            if level > 0:
                x_real = x_real - carry[:, :256]
                x_imag = x_imag - carry[:, 256:]
            if level < 2:
                yield
            d_real = leader * (weight_real * dia_v[level, 0] - weight_imag * dia_v[level, 1])
            d_imag = leader * (weight_real * dia_v[level, 1] + weight_imag * dia_v[level, 0])
            if level < 2:
                x_high, x_low = split(jnp.concatenate([x_real, x_imag], axis=1))
                round_high, round_low = split(turned(x_real, x_imag))
                w_both = dot_exact_left(p_t[level], round_high, round_low)
                y_real = d_real - w_both[:, :256]
                y_imag = d_imag - w_both[:, 256:]
                if level > 0:
                    y_real = y_real - back[:, :256]
                    y_imag = y_imag - back[:, 256:]
            else:
                columns = jnp.concatenate([x_imag, -x_real], axis=0)
                col_high, col_low = split(columns)
                y_imag = d_imag - dot_exact_left(p_t[level], col_high, col_low) - back[:, 256:]
            for to in range(NQ):
                sent[level, to, 0] = y_imag[32 * to : 32 * to + 32]
            each(NQ - 1, lambda i, level=level: send_q(level, 0, i).start())
            for to in range(NQ):
                sent[level, to, 1] = x_imag[32 * to : 32 * to + 32]
            each(NQ - 1, lambda i, level=level: send_q(level, 1, i).start())
            if level < 2:
                yield
                q_pieces = (q_big[level, 0], q_big[level, 1])
                carry = dot_split((x_high, x_low), q_pieces)
                yield
                follow = dot_exact_left(p_t[level + 1], round_high, round_low)
                mix = dot_split(split(jnp.concatenate([y_real, y_imag], axis=1)), q_pieces)
                z_real = -(follow[:, :256].T + mix[:, :256])
                z_imag = -(follow[:, 256:].T + mix[:, 256:])
                yield
                back = dot_split((q_t[level, 0], q_t[level, 1]), split(turned(z_real, z_imag)))
                yield

    ready = prepare()
    work = chain()
    for step in PLAN:
        if step == "p":
            next(ready, None)
        elif step == "c":
            next(work, None)
        else:
            half, distance, level = "ot".index(step[0]), int(step[1]), int(step[2])
            if distance == 1:
                wait_zh(level)
            else:
                arrive(level, half, distance - 1)
            push(level, half, distance)
    for _ in ready:
        pass
    for _ in work:
        pass

    def sum_q(level, kind):
        def wait_q(i):
            source = lax.rem(q + 1 + i, NQ)
            remote(
                sent.at[level, 0, kind], got.at[level, source, kind], ab_send.at[level, kind, i],
                ab_recv.at[level, kind, source], x=source // NC, core=lax.rem(source, NC),
            ).wait_recv()

        each(NQ - 1, wait_q)
        got[level, q, kind] = sent[level, q, kind]
        total = got[level, 0, kind]
        for source in range(1, NQ):
            total = total + got[level, source, kind]
        return total

    def send_zr(group, i):
        to = lax.rem(z + 1 + i, NZ)
        return remote(
            z_sent[group].at[to], z_got[group].at[z], zr_send.at[group, i], zr_recv.at[group, z],
            zl=lax.rem(to, NZL), zh=to // NZL,
        )

    def send_yg(group, i):
        return remote(
            y_got[group].at[y], y_got[group].at[y], yg_send.at[group, i], yg_recv.at[group, y],
            y=lax.rem(y + 1 + i, NY),
        )

    def send_zg(group, i):
        to = lax.rem(z + 1 + i, NZ)
        place = whole[group].at[q, z]
        return remote(
            place, place, zg_send.at[group, i], zg_recv.at[group, z], zl=lax.rem(to, NZL), zh=to // NZL
        )

    def send_fx(group, i):
        place = whole[group].at[q]
        return remote(place, place, fx_send.at[group, i], f_recv.at[group, q], x=lax.rem(x + 1 + i, NX))

    def send_fc(group, i):
        block = lax.rem(x + i, NX) * NC + core
        place = whole[group].at[block]
        return remote(place, place, fc_send.at[group, i], f_recv.at[group, block], core=1 - core)

    def wait_f(group, block, i):
        place = whole[group].at[block]
        remote(place, place, fc_send.at[group, i], f_recv.at[group, block], core=1 - core).wait_recv()

    def across_z(group):
        for place, level in enumerate(GROUPS[group]):
            total = sum_q(level, 0)
            for tile in range(NZ):
                row, column = 8 * (tile // 2), 128 * (tile % 2)
                z_sent[group][tile, place] = total[row : row + 8, column : column + 128]
        each(NZ - 1, lambda i: send_zr(group, i).start())

    def across_y(group):
        def wait_zr(i):
            source = lax.rem(z + 1 + i, NZ)
            remote(
                z_sent[group].at[0], z_got[group].at[source], zr_send.at[group, i], zr_recv.at[group, source],
                zl=lax.rem(source, NZL), zh=source // NZL,
            ).wait_recv()

        each(NZ - 1, wait_zr)
        z_got[group][z] = z_sent[group][z]
        total = z_got[group][0]
        for source in range(1, NZ):
            total = total + z_got[group][source]
        y_got[group][y] = total
        each(NY - 1, lambda i: send_yg(group, i).start())

    def back_z(group):
        def wait_yg(i):
            source = lax.rem(y + 1 + i, NY)
            place = y_got[group].at[source]
            remote(place, place, yg_send.at[group, i], yg_recv.at[group, source], y=source).wait_recv()

        each(NY - 1, wait_yg)
        total = y_got[group][0]
        for source in range(1, NY):
            total = total + y_got[group][source]
        whole[group][q, z] = total
        each(NZ - 1, lambda i: send_zg(group, i).start())

    def back_x(group):
        def wait_zg(i):
            source = lax.rem(z + 1 + i, NZ)
            place = whole[group].at[q, source]
            remote(
                place, place, zg_send.at[group, i], zg_recv.at[group, source],
                zl=lax.rem(source, NZL), zh=source // NZL,
            ).wait_recv()

        each(NZ - 1, wait_zg)
        each(NX - 1, lambda i: send_fx(group, i).start())
        send_fc(group, 0).start()

    def back_core(group):
        def relay(i):
            wait_f(group, lax.rem(x + 1 + i, NX) * NC + core, 1 + i)
            send_fc(group, 1 + i).start()

        each(NX - 1, relay)

    def place_diag(group):
        each(NX, lambda i: wait_f(group, lax.rem(x + i, NX) * NC + (1 - core), i))
        for place, level in enumerate(GROUPS[group]):
            for source in range(NQ):
                for tile in range(NZ):
                    row, column = 32 * source + 8 * (tile // 2), 128 * (tile % 2)
                    diag_out[level, row : row + 8, column : column + 128] = whole[group][source, tile, place]

    def send_p(i):
        to = lax.rem(pole + 1 + i, NP)
        return remote(
            pole_sent.at[to], pole_got.at[pole], p_send.at[i], p_recv.at[pole],
            zl=to // NC, core=lax.rem(to, NC),
        )

    def wait_p(i):
        source = lax.rem(pole + 1 + i, NP)
        remote(
            pole_sent.at[0], pole_got.at[source], p_send.at[i], p_recv.at[source],
            zl=source // NC, core=lax.rem(source, NC),
        ).wait_recv()

    def both(stage):
        for group in range(2):
            stage(group)

    both(across_z)
    both(across_y)
    panel_sums = [sum_q(level, 1) for level in range(3)] + [jnp.zeros((32, 256), F32)]
    pole_sent[...] = jnp.concatenate(panel_sums, axis=0).T.reshape(NP, 32, 128)
    each(NP - 1, lambda i: send_p(i).start())
    both(back_z)
    each(NP - 1, wait_p)
    pole_got[pole] = pole_sent[pole]
    for half in range(NC):
        total = pole_got[half]
        for layer in range(1, NZL):
            total = total + pole_got[layer * NC + half]
        for level in range(3):
            panel_out[level, :, 32 * half : 32 * half + 32] = total[:, 32 * level : 32 * level + 32]
    both(back_x)
    both(back_core)
    both(place_diag)

    for level in range(3):
        send_zh(level).wait_send()

        for kind in range(2):
            each(NQ - 1, lambda i, level=level, kind=kind: send_q(level, kind, i).wait_send())
        for half in range(2):
            for distance in range(1, 5):
                for way in range(2):
                    hop(level, way, half, distance, distance - 1).wait_send()
        each(NX - 1, lambda i, level=level: send_x(level, i).wait_send())

    each(NP - 1, lambda i: send_p(i).wait_send())
    for group in range(2):

        def drain(i, group=group):
            send_zr(group, i).wait_send()
            send_yg(group, i).wait_send()
            send_zg(group, i).wait_send()

        each(NZ - 1, drain)
        each(NX - 1, lambda i, group=group: send_fx(group, i).wait_send())
        each(NX, lambda i, group=group: send_fc(group, i).wait_send())


def per_device(inverse_block, panels, panel_mask, parent_panels, diag_inverse, pole_weights):
    any_space = pl.BlockSpec(memory_space=pl.ANY)
    vmem = pl.BlockSpec(memory_space=pltpu.VMEM)
    smem = pl.BlockSpec(memory_space=pltpu.SMEM)
    dma = pltpu.SemaphoreType.DMA
    panel, diag = pl.pallas_call(
        kernel,
        out_shape=(
            jax.ShapeDtypeStruct((3, 32, 64), F32),
            jax.ShapeDtypeStruct((3, 256, 256), F32),
        ),
        in_specs=[any_space, vmem, smem, any_space, any_space, smem],
        out_specs=(vmem, vmem),
        scratch_shapes=[
            pltpu.VMEM((2, NA, 64, 256), BF16),
            pltpu.VMEM((256, 2048), BF16),
            pltpu.VMEM((2, 2, 256, 256), F32),
            pltpu.VMEM((3, 2, 256, 256), F32),
            pltpu.VMEM((3, NA, 2, 64, 256), BF16),
            pltpu.VMEM((3, NX, 2, 64, 256), BF16),
            pltpu.VMEM((3, 256, 512), BF16),
            pltpu.VMEM((2, 2, 512, 512), BF16),
            pltpu.VMEM((2, 2, 256, 512), BF16),
            pltpu.VMEM((3, NQ, 2, 32, 256), F32),
            pltpu.VMEM((3, NQ, 2, 32, 256), F32),
            pltpu.VMEM((NP, 32, 128), F32),
            pltpu.VMEM((NP, 32, 128), F32),
            pltpu.VMEM((NZ, 2, 8, 128), F32),
            pltpu.VMEM((NZ, 1, 8, 128), F32),
            pltpu.VMEM((NZ, 2, 8, 128), F32),
            pltpu.VMEM((NZ, 1, 8, 128), F32),
            pltpu.VMEM((NY, 2, 8, 128), F32),
            pltpu.VMEM((NY, 1, 8, 128), F32),
            pltpu.VMEM((NQ, NZ, 2, 8, 128), F32),
            pltpu.VMEM((NQ, NZ, 1, 8, 128), F32),
            dma((3,)), dma((48,)), dma((48,)), dma((3,)), dma((3,)), dma((3, NX)), dma((3, NX)),
            dma((3, 2, NQ)), dma((3, 2, NQ)), dma((NP,)), dma((NP,)), dma((2, NZ)), dma((2, NZ)),
            dma((2, NY)), dma((2, NY)), dma((2, NZ)), dma((2, NZ)), dma((2, NX)), dma((2, NX)), dma((2, NQ)),
        ],
        compiler_params=pltpu.CompilerParams(collective_id=0, has_side_effects=True),
    )(
        inverse_block[0, :, :, 0],
        panels[0, :, :, 0, 0],
        panel_mask[:, 0, 0],
        parent_panels[0],
        diag_inverse[0],
        pole_weights[0],
    )
    return panel.swapaxes(1, 2)[:, None, None], diag


def solution(mesh):
    torus = Mesh(
        mesh.devices.reshape(NZL, NC, NX, NY, NZH), ("zl", "core", "x", "y", "zh")
    )
    placed = (
        P(POLE, None, None, "x", None, COL),
        P(POLE, None, None, COL, "x", None, None),
        P(None, COL, "x"),
        P(POLE, None, None, None, None),
        P(POLE, None, None, None, None),
        P(POLE, None),
    )
    return jax.shard_map(
        per_device,
        mesh=torus,
        in_specs=placed,
        out_specs=(P(None, COL, "x", None, POLE), P()),
        check_vma=False,
    )
```

```python
import jax
import jax.numpy as jnp
from jax import lax
from jax.experimental import pallas as pl
from jax.experimental.pallas import tpu as pltpu
from jax.sharding import Mesh
from jax.sharding import PartitionSpec as P

F32 = jnp.float32
BF16 = jnp.bfloat16
MESH = pl.DeviceIdType.MESH
POLE = ("zl", "core")
COL = ("y", "zh")
NZL, NC, NX, NY, NZH = 4, 2, 4, 8, 2
NZ = NZL * NZH
NQ = NX * NC
NP = NZL * NC
NA = NY * NZH
GROUPS = ((0, 1), (2,))

PLAN = (
    "o20", "p", "o21", "p", "t10", "p", "o30", "p", "o22", "p", "t20", "p", "t11", "p", "o31", "p", "t30",
    "p", "o40", "p", "t12", "p", "t40", "t21", "o32", "o41", "t22", "c", "t31", "c", "o42", "c", "t32", "c",
    "c", "t41", "c", "t42", "c", "c",
)


def split(value):
    high = value.astype(BF16)
    low = (value - high.astype(F32)).astype(BF16)
    return high, low


def dot(left, right):
    return lax.dot_general(left, right, (((1,), (0,)), ((), ())), preferred_element_type=F32)


def dot_exact_left(left, right_high, right_low):
    return dot(left, right_high) + dot(left, right_low)


def dot_split(left, right):
    return dot(left[0], right[0]) + (dot(left[1], right[0]) + dot(left[0], right[1]))


def turned(real, imag):
    upper = jnp.concatenate([real, imag], axis=1)
    lower = jnp.concatenate([imag, -real], axis=1)
    return jnp.concatenate([upper, lower], axis=0)


def kernel(
    inv_ref, pan_ref, mask_ref, par_ref, dia_ref, weight_ref,
    panel_out, diag_out,
    g_in, g_t, par_v, dia_v, gath, near, p_t, q_big, q_t, sent, got,
    pole_sent, pole_got, z_sent_early, z_sent_late, z_got_early, z_got_late,
    y_got_early, y_got_late, whole_early, whole_late,
    load_sem, y_send, y_recv, zh_send, zh_recv, x_send, x_recv, ab_send, ab_recv,
    p_send, p_recv, zr_send, zr_recv, yg_send, yg_recv, zg_send, zg_recv,
    fx_send, fc_send, f_recv,
):
    zl = lax.axis_index("zl")
    core = lax.axis_index("core")
    x = lax.axis_index("x")
    y = lax.axis_index("y")
    zh = lax.axis_index("zh")
    z = zh * NZL + zl
    q = x * NC + core
    pole = zl * NC + core
    own = y * NZH + zh
    other = y * NZH + (1 - zh)

    def remote(source, target, send, recv, **where):
        return pltpu.make_async_remote_copy(
            src_ref=source, dst_ref=target, send_sem=send, recv_sem=recv,
            device_id=where, device_id_type=MESH,
        )

    def each(count, body):
        def step(index, carry):
            body(index)
            return carry
        lax.fori_loop(0, count, step, 0)

    z_sent = (z_sent_early, z_sent_late)
    z_got = (z_got_early, z_got_late)
    y_got = (y_got_early, y_got_late)
    whole = (whole_early, whole_late)

    loads = [
        pltpu.make_async_copy(inv_ref, g_in, load_sem.at[0]),
        pltpu.make_async_copy(par_ref, par_v, load_sem.at[1]),
        pltpu.make_async_copy(dia_ref, dia_v, load_sem.at[2]),
    ]
    for load in loads:
        load.start()

    barrier = pltpu.get_barrier_semaphore()

    def greet(**where):
        pl.semaphore_signal(barrier, inc=1, device_id=where, device_id_type=MESH)

    each(NY - 1, lambda i: greet(y=lax.rem(y + 1 + i, NY)))

    def greet_z(i):
        to = lax.rem(z + 1 + i, NZ)
        greet(zl=lax.rem(to, NZL), zh=to // NZL)

    each(NZ - 1, greet_z)

    def greet_q(i):
        to = lax.rem(q + 1 + i, NQ)
        greet(x=to // NC, core=lax.rem(to, NC))

    each(NQ - 1, greet_q)
    each(NZL - 1, lambda i: greet(zl=lax.rem(zl + 1 + i, NZL), core=1 - core))

    for level in range(3):
        flag = mask_ref[level].astype(F32)
        for part in range(2):
            block = (pan_ref[level, part].astype(F32) * flag).astype(BF16)
            gath[level, own, part] = block
            near[level, x, part] = block

    pl.semaphore_wait(barrier, NY - 1 + NZ - 1 + NQ - 1 + NZL - 1)

    def send_zh(level):
        return remote(
            gath.at[level, own], gath.at[level, own], zh_send.at[level], zh_recv.at[level], zh=1 - zh
        )

    def wait_zh(level):
        remote(
            gath.at[level, other], gath.at[level, other], zh_send.at[level], zh_recv.at[level], zh=1 - zh
        ).wait_recv()

    def hop(level, way, half, distance, behind):
        source = lax.rem(y + (behind if way else NY - behind), NY)
        block = source * NZH + (1 - zh if half else zh)
        place = gath.at[level, block] if distance < 4 else gath.at[level, block, way]
        index = ((level * 2 + way) * 2 + half) * 4 + distance - 1
        return remote(
            place, place, y_send.at[index], y_recv.at[index], y=lax.rem(y + (NY - 1 if way else 1), NY)
        )

    def arrive(level, half, distance):
        for way in range(2):
            hop(level, way, half, distance, distance).wait_recv()

    def push(level, half, distance):
        for way in range(2):
            hop(level, way, half, distance, distance - 1).start()

    def send_x(level, i):
        return remote(
            near.at[level, x], near.at[level, x], x_send.at[level, i], x_recv.at[level, x],
            x=lax.rem(x + 1 + i, NX),
        )

    for level in range(3):
        send_zh(level).start()
        push(level, 0, 1)
    for level in range(3):
        each(NX - 1, lambda i, level=level: send_x(level, i).start())

    def send_q(level, kind, i):
        to = lax.rem(q + 1 + i, NQ)
        return remote(
            sent.at[level, to, kind], got.at[level, q, kind], ab_send.at[level, kind, i], ab_recv.at[level, kind, q],
            x=to // NC, core=lax.rem(to, NC),
        )

    weight_real = weight_ref[0]
    weight_imag = weight_ref[1]
    first = (x == 0) & (y == 0) & (zh == 0)
    leader = jnp.where(first, 1.0, 0.0).astype(F32)

    def wait_x(level, i):
        source = lax.rem(x + 1 + i, NX)
        remote(
            near.at[level, source], near.at[level, source], x_send.at[level, i], x_recv.at[level, source], x=source
        ).wait_recv()

    def prepare():
        for load in loads:
            load.wait()
        for part in range(2):
            for piece in range(4):
                g_t[:, part * 1024 + piece * 256 : part * 1024 + piece * 256 + 256] = (
                    g_in[part, 4 * piece : 4 * piece + 4].reshape(256, 256).T
                )
                if piece % 2:
                    yield
        for step in range(2):
            real = split(par_v[step, 0])
            imag = split(par_v[step, 1])
            for piece in range(2):
                q_big[step, piece, :256, :256] = real[piece]
                q_big[step, piece, :256, 256:] = imag[piece]
                q_big[step, piece, 256:, :256] = -imag[piece]
                q_big[step, piece, 256:, 256:] = real[piece]
                q_t[step, piece, :, :256] = real[piece].T
                q_t[step, piece, :, 256:] = -imag[piece].T
                yield
        for level in range(3):
            each(NX - 1, lambda i, level=level: wait_x(level, i))
            p_t[level, :, :256] = near[level, :, 0].reshape(256, 256).T
            p_t[level, :, 256:] = -(near[level, :, 1].reshape(256, 256).T)
            yield

    def chain():
        carry = None
        back = None
        for level in range(3):
            for half in range(2):
                arrive(level, half, 4)
            p_real = gath[level, :, 0].reshape(1024, 256)
            p_imag = gath[level, :, 1].reshape(1024, 256)
            g_real = g_t[:, :1024]
            g_imag = g_t[:, 1024:]
            b_real = dot(g_real, p_real) - dot(g_imag, p_imag)
            if level < 2:
                yield
            b_imag = dot(g_real, p_imag) + dot(g_imag, p_real)
            x_real = -(weight_real * b_real - weight_imag * b_imag)
            x_imag = -(weight_real * b_imag + weight_imag * b_real)
            if level > 0:
                x_real = x_real - carry[:, :256]
                x_imag = x_imag - carry[:, 256:]
            if level < 2:
                yield
            d_real = leader * (weight_real * dia_v[level, 0] - weight_imag * dia_v[level, 1])
            d_imag = leader * (weight_real * dia_v[level, 1] + weight_imag * dia_v[level, 0])
            if level < 2:
                x_high, x_low = split(jnp.concatenate([x_real, x_imag], axis=1))
                round_high, round_low = split(turned(x_real, x_imag))
                w_both = dot_exact_left(p_t[level], round_high, round_low)
                y_real = d_real - w_both[:, :256]
                y_imag = d_imag - w_both[:, 256:]
                if level > 0:
                    y_real = y_real - back[:, :256]
                    y_imag = y_imag - back[:, 256:]
            else:
                columns = jnp.concatenate([x_imag, -x_real], axis=0)
                col_high, col_low = split(columns)
                y_imag = d_imag - dot_exact_left(p_t[level], col_high, col_low) - back[:, 256:]
            for to in range(NQ):
                sent[level, to, 0] = y_imag[32 * to : 32 * to + 32]
            each(NQ - 1, lambda i, level=level: send_q(level, 0, i).start())
            for to in range(NQ):
                sent[level, to, 1] = x_imag[32 * to : 32 * to + 32]
            for due in ((0,), (), (1, 2))[level]:
                each(NQ - 1, lambda i, due=due: send_q(due, 1, i).start())
            if level < 2:
                yield
                q_pieces = (q_big[level, 0], q_big[level, 1])
                carry = dot_split((x_high, x_low), q_pieces)
                yield
                follow = dot_exact_left(p_t[level + 1], round_high, round_low)
                mix = dot_split(split(jnp.concatenate([y_real, y_imag], axis=1)), q_pieces)
                z_real = -(follow[:, :256].T + mix[:, :256])
                z_imag = -(follow[:, 256:].T + mix[:, 256:])
                yield
                back = dot_split((q_t[level, 0], q_t[level, 1]), split(turned(z_real, z_imag)))
                yield

    ready = prepare()
    work = chain()
    for step in PLAN:
        if step == "p":
            next(ready, None)
        elif step == "c":
            next(work, None)
        else:
            half, distance, level = "ot".index(step[0]), int(step[1]), int(step[2])
            if distance == 1:
                wait_zh(level)
            else:
                arrive(level, half, distance - 1)
            push(level, half, distance)
    for _ in ready:
        pass
    for _ in work:
        pass

    def sum_q(level, kind):
        def wait_q(i):
            source = lax.rem(q + 1 + i, NQ)
            remote(
                sent.at[level, 0, kind], got.at[level, source, kind], ab_send.at[level, kind, i],
                ab_recv.at[level, kind, source], x=source // NC, core=lax.rem(source, NC),
            ).wait_recv()

        each(NQ - 1, wait_q)
        got[level, q, kind] = sent[level, q, kind]
        total = got[level, 0, kind]
        for source in range(1, NQ):
            total = total + got[level, source, kind]
        return total

    def send_zr(group, i):
        to = lax.rem(z + 1 + i, NZ)
        return remote(
            z_sent[group].at[to], z_got[group].at[z], zr_send.at[group, i], zr_recv.at[group, z],
            zl=lax.rem(to, NZL), zh=to // NZL,
        )

    def send_yg(group, i):
        return remote(
            y_got[group].at[y], y_got[group].at[y], yg_send.at[group, i], yg_recv.at[group, y],
            y=lax.rem(y + 1 + i, NY),
        )

    def send_zg(group, i):
        to = lax.rem(z + 1 + i, NZ)
        place = whole[group].at[q, z]
        return remote(
            place, place, zg_send.at[group, i], zg_recv.at[group, z], zl=lax.rem(to, NZL), zh=to // NZL
        )

    def send_fx(group, i):
        place = whole[group].at[q]
        return remote(place, place, fx_send.at[group, i], f_recv.at[group, q], x=lax.rem(x + 1 + i, NX))

    def send_fc(group, i):
        block = lax.rem(x + i, NX) * NC + core
        place = whole[group].at[block]
        return remote(place, place, fc_send.at[group, i], f_recv.at[group, block], core=1 - core)

    def wait_f(group, block, i):
        place = whole[group].at[block]
        remote(place, place, fc_send.at[group, i], f_recv.at[group, block], core=1 - core).wait_recv()

    def across_z(group):
        for place, level in enumerate(GROUPS[group]):
            total = sum_q(level, 0)
            for tile in range(NZ):
                row, column = 8 * (tile // 2), 128 * (tile % 2)
                z_sent[group][tile, place] = total[row : row + 8, column : column + 128]
        each(NZ - 1, lambda i: send_zr(group, i).start())

    def across_y(group):
        def wait_zr(i):
            source = lax.rem(z + 1 + i, NZ)
            remote(
                z_sent[group].at[0], z_got[group].at[source], zr_send.at[group, i], zr_recv.at[group, source],
                zl=lax.rem(source, NZL), zh=source // NZL,
            ).wait_recv()

        each(NZ - 1, wait_zr)
        z_got[group][z] = z_sent[group][z]
        total = z_got[group][0]
        for source in range(1, NZ):
            total = total + z_got[group][source]
        y_got[group][y] = total
        each(NY - 1, lambda i: send_yg(group, i).start())

    def back_z(group):
        def wait_yg(i):
            source = lax.rem(y + 1 + i, NY)
            place = y_got[group].at[source]
            remote(place, place, yg_send.at[group, i], yg_recv.at[group, source], y=source).wait_recv()

        each(NY - 1, wait_yg)
        total = y_got[group][0]
        for source in range(1, NY):
            total = total + y_got[group][source]
        whole[group][q, z] = total
        each(NZ - 1, lambda i: send_zg(group, i).start())

    def back_x(group):
        def wait_zg(i):
            source = lax.rem(z + 1 + i, NZ)
            place = whole[group].at[q, source]
            remote(
                place, place, zg_send.at[group, i], zg_recv.at[group, source],
                zl=lax.rem(source, NZL), zh=source // NZL,
            ).wait_recv()

        each(NZ - 1, wait_zg)
        each(NX - 1, lambda i: send_fx(group, i).start())
        send_fc(group, 0).start()

    def back_core(group):
        def relay(i):
            wait_f(group, lax.rem(x + 1 + i, NX) * NC + core, 1 + i)
            send_fc(group, 1 + i).start()

        each(NX - 1, relay)

    def place_diag(group):
        each(NX, lambda i: wait_f(group, lax.rem(x + i, NX) * NC + (1 - core), i))
        for place, level in enumerate(GROUPS[group]):
            for source in range(NQ):
                for tile in range(NZ):
                    row, column = 32 * source + 8 * (tile // 2), 128 * (tile % 2)
                    diag_out[level, row : row + 8, column : column + 128] = whole[group][source, tile, place]

    def send_p(i):
        to = lax.rem(pole + 1 + i, NP)
        return remote(
            pole_sent.at[to], pole_got.at[pole], p_send.at[i], p_recv.at[pole],
            zl=to // NC, core=lax.rem(to, NC),
        )

    def wait_p(i):
        source = lax.rem(pole + 1 + i, NP)
        remote(
            pole_sent.at[0], pole_got.at[source], p_send.at[i], p_recv.at[source],
            zl=source // NC, core=lax.rem(source, NC),
        ).wait_recv()

    def both(stage):
        for group in range(2):
            stage(group)

    both(across_z)
    both(across_y)
    both(back_z)
    panel_sums = [sum_q(level, 1) for level in range(3)] + [jnp.zeros((32, 256), F32)]
    pole_sent[...] = jnp.concatenate(panel_sums, axis=0).T.reshape(NP, 32, 128)
    each(NP - 1, lambda i: send_p(i).start())
    both(back_x)
    each(NP - 1, wait_p)
    pole_got[pole] = pole_sent[pole]
    for half in range(NC):
        total = pole_got[half]
        for layer in range(1, NZL):
            total = total + pole_got[layer * NC + half]
        for level in range(3):
            panel_out[level, :, 32 * half : 32 * half + 32] = total[:, 32 * level : 32 * level + 32]
    both(back_core)
    both(place_diag)

    for level in range(3):
        send_zh(level).wait_send()

        for kind in range(2):
            each(NQ - 1, lambda i, level=level, kind=kind: send_q(level, kind, i).wait_send())
        for half in range(2):
            for distance in range(1, 5):
                for way in range(2):
                    hop(level, way, half, distance, distance - 1).wait_send()
        each(NX - 1, lambda i, level=level: send_x(level, i).wait_send())

    each(NP - 1, lambda i: send_p(i).wait_send())
    for group in range(2):

        def drain(i, group=group):
            send_zr(group, i).wait_send()
            send_yg(group, i).wait_send()
            send_zg(group, i).wait_send()

        each(NZ - 1, drain)
        each(NX - 1, lambda i, group=group: send_fx(group, i).wait_send())
        each(NX, lambda i, group=group: send_fc(group, i).wait_send())


def per_device(inverse_block, panels, panel_mask, parent_panels, diag_inverse, pole_weights):
    any_space = pl.BlockSpec(memory_space=pl.ANY)
    vmem = pl.BlockSpec(memory_space=pltpu.VMEM)
    smem = pl.BlockSpec(memory_space=pltpu.SMEM)
    dma = pltpu.SemaphoreType.DMA
    panel, diag = pl.pallas_call(
        kernel,
        out_shape=(
            jax.ShapeDtypeStruct((3, 32, 64), F32),
            jax.ShapeDtypeStruct((3, 256, 256), F32),
        ),
        in_specs=[any_space, vmem, smem, any_space, any_space, smem],
        out_specs=(vmem, vmem),
        scratch_shapes=[
            pltpu.VMEM((2, NA, 64, 256), BF16),
            pltpu.VMEM((256, 2048), BF16),
            pltpu.VMEM((2, 2, 256, 256), F32),
            pltpu.VMEM((3, 2, 256, 256), F32),
            pltpu.VMEM((3, NA, 2, 64, 256), BF16),
            pltpu.VMEM((3, NX, 2, 64, 256), BF16),
            pltpu.VMEM((3, 256, 512), BF16),
            pltpu.VMEM((2, 2, 512, 512), BF16),
            pltpu.VMEM((2, 2, 256, 512), BF16),
            pltpu.VMEM((3, NQ, 2, 32, 256), F32),
            pltpu.VMEM((3, NQ, 2, 32, 256), F32),
            pltpu.VMEM((NP, 32, 128), F32),
            pltpu.VMEM((NP, 32, 128), F32),
            pltpu.VMEM((NZ, 2, 8, 128), F32),
            pltpu.VMEM((NZ, 1, 8, 128), F32),
            pltpu.VMEM((NZ, 2, 8, 128), F32),
            pltpu.VMEM((NZ, 1, 8, 128), F32),
            pltpu.VMEM((NY, 2, 8, 128), F32),
            pltpu.VMEM((NY, 1, 8, 128), F32),
            pltpu.VMEM((NQ, NZ, 2, 8, 128), F32),
            pltpu.VMEM((NQ, NZ, 1, 8, 128), F32),
            dma((3,)), dma((48,)), dma((48,)), dma((3,)), dma((3,)), dma((3, NX)), dma((3, NX)),
            dma((3, 2, NQ)), dma((3, 2, NQ)), dma((NP,)), dma((NP,)), dma((2, NZ)), dma((2, NZ)),
            dma((2, NY)), dma((2, NY)), dma((2, NZ)), dma((2, NZ)), dma((2, NX)), dma((2, NX)), dma((2, NQ)),
        ],
        compiler_params=pltpu.CompilerParams(collective_id=0, has_side_effects=True),
    )(
        inverse_block[0, :, :, 0],
        panels[0, :, :, 0, 0],
        panel_mask[:, 0, 0],
        parent_panels[0],
        diag_inverse[0],
        pole_weights[0],
    )
    return panel.swapaxes(1, 2)[:, None, None], diag


def solution(mesh):
    torus = Mesh(
        mesh.devices.reshape(NZL, NC, NX, NY, NZH), ("zl", "core", "x", "y", "zh")
    )
    placed = (
        P(POLE, None, None, "x", None, COL),
        P(POLE, None, None, COL, "x", None, None),
        P(None, COL, "x"),
        P(POLE, None, None, None, None),
        P(POLE, None, None, None, None),
        P(POLE, None),
    )
    return jax.shard_map(
        per_device,
        mesh=torus,
        in_specs=placed,
        out_specs=(P(None, COL, "x", None, POLE), P()),
        check_vma=False,
    )
```
